256 devices in a mesh: freq: 8 (over y, z_hi), dom: 32 (over x, z_lo, core).
Axes of the slice: x: 4, y: 4, z: 8 (z_hi: 2, z_lo: 4; z = z_hi * 4 + z_lo), core: 2. Of those that a mesh axis runs over, the one named last changes fastest.
Arguments:
- fwd_source: float32 [16, 4, 1024, 128], P('freq', None, 'dom'), may hold values from -6 to 6
- adj_source: float32 [16, 4, 1024, 128], P('freq', None, 'dom'), may hold values from -6 to 6
- curl_blocks: float32 [1024, 4, 128, 128], P('dom')
- block_links: int32 [1024, 4], P('dom'), may hold values from 0 to 95, as said below
- tile_lists: int32 [128, 16], P('dom'), may hold values from 0 to 31, as said below
- edge_mass: float32 [1024, 128], P('dom'), may hold values from 0.5 to 1.5
- omega: float32 [16], P('freq'), may hold values from 0.1 to 1
- cell_edges: int32 [12, 32768], P(None, 'dom'), may hold values from 0 to 4095
- log_cond: float32 [32768], P('dom'), may hold values from -6 to 6
Outputs:
- fwd_field: float32 [16, 4, 1024, 128], P('freq', None, 'dom')
- adj_field: float32 [16, 4, 1024, 128], P('freq', None, 'dom')
- model_next: float32 [32768], P('dom')
The draws below stay inside these ranges and needn't reach their ends.
Inputs may be any that keep to these rules, and one draw needn't show every extreme that they name: `block_links`: entry 0 of each block row is the row's own local block; the others index the partition's extended field, local blocks first, then the tiles received in round 0, 1 and so on; every received tile is referenced by some row of the partition. `tile_lists`: the 16 blocks of one row are distinct local blocks.
All inputs are finite; a program needn't handle non-finite values.
Results may differ from the reference program's by a relative error of at most 0.0001.
Values sent between devices are 32-bit elements; how exact they have to be, the bound alone decides.
No kernel may reach another device: no remote copies, remote signals or barrier semaphores. Data moves between devices by JAX's collectives and lax.ppermute only.
A program may use at most 64 MiB of HBM per device.

```python
import math
import jax
import jax.numpy as jnp
from jax import lax

EB = 128
LINKS = 4
ROUNDS = 4
ITERS = 3
NB = 32
CELLS_DEV = 1024
TILES = 16
NFREQ = 16
BLOCKS = 1024
CELLS = 32768
N_DOM = 32


def draw_curl_blocks(key, part):
    noise = jax.random.normal(key, (BLOCKS, LINKS, EB, EB), jnp.float32)
    noise = noise * (0.25 / jnp.sqrt(1.0 * EB))
    eye = jnp.eye(EB, dtype=jnp.float32)
    first = (jnp.arange(LINKS) == 0).astype(jnp.float32)
    return noise + first[None, :, None, None] * eye[None, None]


def links_of_partition(key):
    slots = ROUNDS * TILES
    entries = NB * (LINKS - 1)
    fill_key, mix_key = jax.random.split(key)
    every = NB + jnp.arange(slots, dtype=jnp.int32)
    extra = jax.random.randint(fill_key, (entries - slots,), 0, NB + slots).astype(jnp.int32)
    mixed = jax.random.permutation(mix_key, jnp.concatenate([every, extra]))
    return mixed.reshape(NB, LINKS - 1)


def draw_block_links(key, part):
    keys = jax.random.split(jax.random.fold_in(key, 11), N_DOM)
    others = jax.vmap(links_of_partition)(keys).reshape(BLOCKS, LINKS - 1)
    own = (jnp.arange(BLOCKS, dtype=jnp.int32) % NB)[:, None]
    return jnp.concatenate([own, others.astype(jnp.int32)], axis=1)


def tiles_of_row(key):
    return jax.random.permutation(key, jnp.arange(NB, dtype=jnp.int32))[:TILES]


def draw_tile_lists(key, part):
    keys = jax.random.split(jax.random.fold_in(key, 23), N_DOM * ROUNDS)
    return jax.vmap(tiles_of_row)(keys).astype(jnp.int32)


def set_ends(values, own_key, least, top_value):
    index_at = [jax.random.randint(jax.random.fold_in(own_key, axis), (), 0, length) for axis, length in enumerate(values.shape)]
    main_axis = values.shape.index(max(values.shape))
    next_to = index_at[:main_axis] + [(index_at[main_axis] + 1) % values.shape[main_axis]] + index_at[main_axis + 1:]
    return values.at[tuple(index_at)].set(least).at[tuple(next_to)].set(top_value)


def levels(own_key, shape, pieces, smallest, top_value):
    loudness = 1.0
    for dim, shards_of in pieces:
        heights = jax.random.uniform(jax.random.fold_in(jax.random.fold_in(own_key, 6), dim), (shards_of,), jnp.float32, smallest / len(pieces), top_value / len(pieces))
        loudness = loudness * jnp.repeat(jnp.exp(heights), shape[dim] // shards_of).reshape((-1,) + (1,) * (len(shape) - 1 - dim))
    return loudness


def bell_draw(stream_key, shape, scale, limit, shards=(), held_as=jnp.bfloat16):
    array = jax.random.normal(stream_key, shape, jnp.float32) * scale
    if len(shards) > 0:
        array = levels(stream_key, shape, shards, -0.22, 0.18) * array
    return jnp.clip(array, min=-limit, max=limit).astype(held_as)


def setup_inputs(seed: int = 0) -> dict:
    splits = jax.random.split(jax.random.key(seed), 10)
    return {
        "fwd_source": bell_draw(splits[0], (NFREQ, 4, BLOCKS, EB), 1.0, 6.0, ((0, 8), (2, 32)), jnp.float32),
        "adj_source": bell_draw(splits[1], (NFREQ, 4, BLOCKS, EB), 1.0, 6.0, ((0, 8), (2, 32)), jnp.float32),
        "curl_blocks": draw_curl_blocks(jax.random.fold_in(splits[9], 71), 0),
        "block_links": draw_block_links(jax.random.fold_in(splits[9], 71), 0),
        "tile_lists": draw_tile_lists(jax.random.fold_in(splits[9], 71), 0),
        "edge_mass": jnp.clip(0.5 + 1.0 * jax.random.uniform(splits[5], (BLOCKS, EB), jnp.float32) ** levels(splits[5], (BLOCKS, EB), ((0, 32),), -0.2, 0.2), 0.5, 1.5),
        "omega": jnp.clip(jnp.exp(math.log(1.0) - 2.3025851 * jax.random.uniform(splits[6], (NFREQ,), jnp.float32) ** levels(splits[6], (NFREQ,), ((0, 8),), -0.2, 0.2)), 0.1, 1.0),
        "cell_edges": set_ends(jax.random.randint(splits[7], (12, CELLS), 0, NB * EB), jax.random.fold_in(splits[7], 1), 0, (NB * EB) - 1).astype(jnp.int32),
        "log_cond": bell_draw(splits[8], (CELLS,), 1.0, 6.0, ((0, 32),), jnp.float32),
    }


def apply_op(u, blocks, links, tiles, mass, omega):
    parts = [u]
    doms = jnp.arange(N_DOM, dtype=jnp.int32)
    for r in range(ROUNDS):
        partner = jnp.bitwise_xor(doms, 1 << r)
        index = tiles[partner, r]
        source = u[:, :, partner]
        got = jnp.take_along_axis(source, index[None, None, :, :, None], axis=3)
        parts.append(got)
    extended = jnp.concatenate(parts, axis=3)
    flat = links.reshape(N_DOM, NB * LINKS)
    gathered = jnp.take_along_axis(extended, flat[None, None, :, :, None], axis=3)
    gathered = gathered.reshape(u.shape[0], 4, N_DOM, NB, LINKS, EB)
    curl = jnp.einsum('dblij,fcdblj->fcdbi', blocks, gathered, precision=lax.Precision.HIGHEST)
    curl = curl.reshape(u.shape[0], 2, 2, N_DOM, NB, EB)
    split = u.reshape(u.shape[0], 2, 2, N_DOM, NB, EB)
    weight = omega[:, None, None, None, None] * mass[None, None]
    real_part = curl[:, :, 0] - weight * split[:, :, 1]
    imag_part = curl[:, :, 1] + weight * split[:, :, 0]
    return jnp.stack([real_part, imag_part], axis=2).reshape(u.shape)

def chebyshev(source, blocks, links, tiles, mass, omega):
    theta = 1.0
    delta = 0.7
    sone = theta / delta
    rho = 1.0 / sone
    solution = jnp.zeros_like(source)
    resid = source
    direction = source / theta
    for step in range(ITERS):
        solution = solution + direction
        if step + 1 < ITERS:
            resid = resid - apply_op(direction, blocks, links, tiles, mass, omega)
            rho_new = 1.0 / (2.0 * sone - rho)
            direction = rho_new * rho * direction + 2.0 * rho_new / delta * resid
            rho = rho_new
    return solution

def reference(fwd_source, adj_source, curl_blocks, block_links, tile_lists, edge_mass, omega, cell_edges, log_cond):
    blocks = curl_blocks.reshape(N_DOM, NB, LINKS, EB, EB)
    links = block_links.reshape(N_DOM, NB, LINKS)
    tiles = tile_lists.reshape(N_DOM, ROUNDS, TILES)
    mass = edge_mass.reshape(N_DOM, NB, EB)
    fwd = fwd_source.reshape(NFREQ, 4, N_DOM, NB, EB)
    adj = adj_source.reshape(NFREQ, 4, N_DOM, NB, EB)
    efield = chebyshev(fwd, blocks, links, tiles, mass, omega)
    lfield = chebyshev(adj, blocks, links, tiles, mass, omega)
    esplit = efield.reshape(NFREQ, 2, 2, N_DOM, NB * EB)
    lsplit = lfield.reshape(NFREQ, 2, 2, N_DOM, NB * EB)
    prod = esplit[:, :, 0] * lsplit[:, :, 1] + esplit[:, :, 1] * lsplit[:, :, 0]
    edge_term = lax.optimization_barrier(jnp.sum(omega[:, None, None, None] * prod, axis=(0, 1)))
    owned = cell_edges.reshape(12, N_DOM, CELLS_DEV).transpose(1, 0, 2).reshape(N_DOM, 12 * CELLS_DEV)
    picked = jnp.take_along_axis(edge_term, owned, axis=1).reshape(N_DOM, 12, CELLS_DEV)
    grad = lax.optimization_barrier(jnp.sum(picked, axis=1)).reshape(CELLS) / jnp.sqrt(24.0 * NFREQ)
    model_next = log_cond - 0.5 * grad / jnp.sqrt(grad * grad + 1.0)
    return (efield.reshape(NFREQ, 4, BLOCKS, EB), lfield.reshape(NFREQ, 4, BLOCKS, EB), model_next)
```

```python
import math

import jax
import jax.numpy as jnp
from jax import lax
from jax.experimental import pallas as pl
from jax.experimental.pallas import tpu as pltpu
from jax.sharding import PartitionSpec as P

THETA = 1.0
DELTA = 0.7
SONE = THETA / DELTA
RHO0 = 1.0 / SONE
RHO1 = 1.0 / (2.0 * SONE - RHO0)
RHO2 = 1.0 / (2.0 * SONE - RHO1)
C1, C2 = RHO1 * RHO0, 2.0 * RHO1 / DELTA
C3, C4 = RHO2 * RHO1, 2.0 * RHO2 / DELTA

F32, BF16 = jnp.float32, jnp.bfloat16
VM = pl.BlockSpec(memory_space=pltpu.VMEM)
SM = pl.BlockSpec(memory_space=pltpu.SMEM)
NT = (((1,), (1,)), ((), ()))


def swapped(value, axis, mask):
    pairs = [(source, source ^ mask) for source in range(lax.axis_size(axis))]
    return lax.ppermute(value, axis, pairs)


def near(value):
    return pltpu.with_memory_space_constraint(value, pltpu.VMEM)


def params(mib):
    return pltpu.CompilerParams(vmem_limit_bytes=mib << 20)


def cost(flops, moved):
    return pl.CostEstimate(flops=flops, bytes_accessed=moved, transcendentals=0)


def halves(value):
    high = value.astype(BF16)
    return high, (value - high.astype(F32)).astype(BF16)


def other(value):
    count = value.shape[0]
    even = lax.broadcasted_iota(jnp.int32, value.shape, 0) % 2 == 0
    return jnp.where(even, pltpu.roll(value, count - 1, 0), pltpu.roll(value, 1, 0))


def frequency_rows(omega_ref, rows, lanes):
    row = lax.broadcasted_iota(jnp.int32, (rows, lanes), 0)
    count = omega_ref.shape[0]
    which = (row // 4) % count
    out = jnp.full((rows, lanes), omega_ref[0], F32)
    for f in range(1, count):
        out = jnp.where(which == f, omega_ref[f], out)
    return out, row % 2 == 0


def pick(tiles_ref, field_ref, send_refs):
    for r, send_ref in enumerate(send_refs):
        for t in range(send_ref.shape[0]):
            send_ref[t] = field_ref[tiles_ref[r, t]]


def prepare(tiles_ref, fwd_ref, adj_ref, field_ref, *send_refs):
    blocks, rows, _ = field_ref.shape
    half = rows // 2
    for b in range(blocks):
        field_ref[b, :half] = fwd_ref[pl.ds(b, half, stride=blocks), :]
        field_ref[b, half:] = adj_ref[pl.ds(b, half, stride=blocks), :]
    pick(tiles_ref, field_ref, send_refs)


def split(curl_ref, high_ref, low_ref, buf, sems):
    blocks, links, width, _ = curl_ref.shape
    copies = [
        pltpu.make_async_copy(curl_ref.at[b], buf.at[b], sems.at[b]) for b in range(blocks)
    ]
    for copy in copies:
        copy.start()
    for b in range(blocks):
        copies[b].wait()
        for k in range(links):
            high, low = halves(buf[b, k])
            high_ref[b, :, k * width : (k + 1) * width] = high
            low_ref[b, :, k * width : (k + 1) * width] = low


def extend(field_ref, got_refs, ext):
    blocks, rows, _ = field_ref.shape
    at = 0
    for ref in (field_ref, *got_refs):
        for t in range(ref.shape[0]):
            high, low = halves(ref[t])
            ext[at, :rows] = high
            ext[at, rows:] = low
            at += 1


def curl_row(b, links_ref, high_ref, low_ref, ext):
    rows = ext.shape[1] // 2
    x = jnp.concatenate([ext[links_ref[k, b]] for k in range(links_ref.shape[0])], axis=1)
    main = lax.dot_general(x, high_ref[b], NT, preferred_element_type=F32)
    rest = lax.dot_general(x[:rows], low_ref[b], NT, preferred_element_type=F32)
    return main[:rows] + (main[rows:] + rest)


def first(
    links_ref, tiles_ref, omega_ref, mass_ref, field_ref, high_ref, low_ref, got1, got2, got3, got4,
    dir_ref, base_ref, send1, send2, send3, send4, ext,
):
    blocks, rows, lanes = field_ref.shape
    extend(field_ref, (got1, got2, got3, got4), ext)
    omega, real = frequency_rows(omega_ref, rows, lanes)
    sign = jnp.where(real, -omega, omega)
    for b in range(blocks):
        u = field_ref[b]
        au = curl_row(b, links_ref, high_ref, low_ref, ext)
        au = au + sign * mass_ref[b : b + 1] * other(u)
        resid = u - au
        direction = C1 * u + C2 * resid
        dir_ref[b] = direction
        base_ref[b] = u + direction + C3 * direction + C4 * resid
    pick(tiles_ref, dir_ref, (send1, send2, send3, send4))


def second(
    scale, links_ref, omega_ref, mass_ref, dir_ref, base_ref, high_ref, low_ref, got1, got2, got3, got4,
    cells_ref, fwd_ref, adj_ref, grad_ref, ext, table,
):
    blocks, rows, lanes = dir_ref.shape
    half = rows // 2
    extend(dir_ref, (got1, got2, got3, got4), ext)
    omega, real = frequency_rows(omega_ref, rows, lanes)
    sign = jnp.where(real, -omega, omega)
    for b in range(blocks):
        au = curl_row(b, links_ref, high_ref, low_ref, ext)
        au = au + sign * mass_ref[b : b + 1] * other(dir_ref[b])
        x = base_ref[b] - C4 * au
        efield, lfield = x[:half], x[half:]
        fwd_ref[pl.ds(b, half, stride=blocks), :] = efield
        adj_ref[pl.ds(b, half, stride=blocks), :] = lfield
        prod = omega[:half] * efield * other(lfield)
        table[b : b + 1] = jnp.sum(prod, axis=0, keepdims=True)
    edges, cells = cells_ref.shape
    padded = -(-edges // 8) * 8
    for c in range(cells // lanes):
        index = cells_ref[:, c * lanes : (c + 1) * lanes]
        fill = jnp.full((padded - edges, lanes), -1, jnp.int32)
        index = jnp.concatenate([index, fill], axis=0)
        total = None
        for e in range(0, padded, 8):
            block, lane = index[e : e + 8] >> 7, index[e : e + 8] & 127
            found = jnp.zeros((8, lanes), F32)
            for b in range(blocks):
                row = jnp.broadcast_to(table[b : b + 1], (8, lanes))
                value = jnp.take_along_axis(row, lane, axis=1, mode="promise_in_bounds")
                found = jnp.where(block == b, value, found)
            total = found if total is None else total + found
        grad_ref[c : c + 1] = jnp.sum(total, axis=0, keepdims=True) * scale


def local(
    fwd_source, adj_source, curl_blocks, block_links, tile_lists, edge_mass, omega, cell_edges, log_cond
):
    count, comps, blocks, lanes = fwd_source.shape
    rounds, tiles = tile_lists.shape
    links = block_links.shape[1]
    half = count * comps
    rows = 2 * half
    field_shape = pltpu.VMEM((blocks, rows, lanes), F32)
    tile_shape = pltpu.VMEM((tiles, rows, lanes), F32)
    matrix_shape = pltpu.VMEM((blocks, lanes, links * lanes), BF16)
    flat = (half * blocks, lanes)
    ext = pltpu.VMEM((blocks + rounds * tiles, 2 * rows, lanes), BF16)
    links_t = block_links.T

    field, *sends = pl.pallas_call(
        prepare,
        out_shape=[field_shape] + [tile_shape] * rounds,
        in_specs=[SM, VM, VM],
        out_specs=[VM] * (1 + rounds),
        compiler_params=params(8),
        name="prepare",
    )(tile_lists, fwd_source.reshape(flat), adj_source.reshape(flat))

    def trade(sends):
        got = [None] * rounds
        for r in (2, 1, 3, 0):
            got[r] = swapped(sends[r], "dom", 2**r)
        return [near(g) for g in got]

    got = trade(sends)
    high, low = pl.pallas_call(
        split,
        out_shape=[matrix_shape] * 2,
        in_specs=[pl.BlockSpec(memory_space=pl.ANY)],
        out_specs=[VM] * 2,
        scratch_shapes=[pltpu.VMEM(curl_blocks.shape, F32), pltpu.SemaphoreType.DMA((blocks,))],
        compiler_params=params(32),
        cost_estimate=cost(8 << 20, 16 << 20),
        name="split",
    )(curl_blocks)
    high, low = near(high), near(low)
    field = near(field)
    direction, base, *sends = pl.pallas_call(
        first,
        out_shape=[field_shape] * 2 + [tile_shape] * rounds,
        in_specs=[SM] * 3 + [VM] * (4 + rounds),
        out_specs=[VM] * (2 + rounds),
        scratch_shapes=[ext],
        compiler_params=params(32),
        name="first",
    )(links_t, tile_lists, omega, edge_mass, field, high, low, *got)
    got = trade(sends)
    scale = 1.0 / math.sqrt(24.0 * count * lax.axis_size("freq"))
    efield, lfield, grad = pl.pallas_call(
        lambda *refs: second(scale, *refs),
        out_shape=[
            jax.ShapeDtypeStruct(flat, F32),
            jax.ShapeDtypeStruct(flat, F32),
            jax.ShapeDtypeStruct((log_cond.shape[0] // lanes, lanes), F32),
        ],
        in_specs=[SM] * 2 + [VM] * (6 + rounds),
        out_specs=[VM] * 3,
        scratch_shapes=[ext, pltpu.VMEM((blocks, lanes), F32)],
        compiler_params=params(32),
        name="second",
    )(links_t, omega, edge_mass, near(direction), near(base), high, low, *got, cell_edges)
    for mask in (2, 6, 1):
        grad = grad + swapped(grad, "freq", mask)
    grad = grad.reshape(log_cond.shape)
    model_next = log_cond - 0.5 * grad / jnp.sqrt(grad * grad + 1.0)
    shape = fwd_source.shape
    return efield.reshape(shape), lfield.reshape(shape), model_next


def solution(mesh):
    field = P("freq", None, "dom", None)
    in_specs = (
        field,
        field,
        P("dom", None, None, None),
        P("dom", None),
        P("dom", None),
        P("dom", None),
        P("freq"),
        P(None, "dom"),
        P("dom"),
    )
    out_specs = (field, field, P("dom"))
    return jax.shard_map(local, mesh=mesh, in_specs=in_specs, out_specs=out_specs, check_vma=False)
```

```python
import math

import jax
import jax.numpy as jnp
from jax import lax
from jax.experimental import pallas as pl
from jax.experimental.pallas import tpu as pltpu
from jax.sharding import PartitionSpec as P

THETA = 1.0
DELTA = 0.7
SONE = THETA / DELTA
RHO0 = 1.0 / SONE
RHO1 = 1.0 / (2.0 * SONE - RHO0)
RHO2 = 1.0 / (2.0 * SONE - RHO1)
C1, C2 = RHO1 * RHO0, 2.0 * RHO1 / DELTA
C3, C4 = RHO2 * RHO1, 2.0 * RHO2 / DELTA

F32, BF16 = jnp.float32, jnp.bfloat16
VM = pl.BlockSpec(memory_space=pltpu.VMEM)
SM = pl.BlockSpec(memory_space=pltpu.SMEM)
HB = pl.BlockSpec(memory_space=pltpu.HBM)
DMA = pltpu.SemaphoreType.DMA
NT = (((1,), (1,)), ((), ()))


def swapped(value, axis, mask):
    pairs = [(source, source ^ mask) for source in range(lax.axis_size(axis))]
    return lax.ppermute(value, axis, pairs)


def near(value):
    return pltpu.with_memory_space_constraint(value, pltpu.VMEM)


def far(value):
    return pltpu.with_memory_space_constraint(value, pltpu.HBM)


def params(mib):
    return pltpu.CompilerParams(vmem_limit_bytes=mib << 20)


def cost(flops, moved):
    return pl.CostEstimate(flops=flops, bytes_accessed=moved, transcendentals=0)


def halves(value):
    high = value.astype(BF16)
    return high, (value - high.astype(F32)).astype(BF16)


def other(value):
    count = value.shape[0]
    even = lax.broadcasted_iota(jnp.int32, value.shape, 0) % 2 == 0
    return jnp.where(even, pltpu.roll(value, count - 1, 0), pltpu.roll(value, 1, 0))


def frequency_rows(omega_ref, rows, lanes):
    row = lax.broadcasted_iota(jnp.int32, (rows, lanes), 0)
    count = omega_ref.shape[0]
    which = (row // 4) % count
    out = jnp.full((rows, lanes), omega_ref[0], F32)
    for f in range(1, count):
        out = jnp.where(which == f, omega_ref[f], out)
    return out, row % 2 == 0


def pick(tiles_ref, field_ref, send_refs):
    for r, send_ref in enumerate(send_refs):
        for t in range(send_ref.shape[0]):
            send_ref[t] = field_ref[tiles_ref[r, t]]


def prepare(
    tiles_hbm, fwd_hbm, adj_hbm, field_ref, send1, send2, send3, send4, tiles_ref, fwd_ref, adj_ref, sems
):
    blocks, rows, _ = field_ref.shape
    half = rows // 2
    pairs = ((tiles_hbm, tiles_ref), (fwd_hbm, fwd_ref), (adj_hbm, adj_ref))
    copies = [pltpu.make_async_copy(a, b, sems.at[i]) for i, (a, b) in enumerate(pairs)]
    for copy in copies:
        copy.start()
    for copy in copies:
        copy.wait()
    for b in range(blocks):
        field_ref[b, :half] = fwd_ref[pl.ds(b, half, stride=blocks), :]
        field_ref[b, half:] = adj_ref[pl.ds(b, half, stride=blocks), :]
    pick(tiles_ref, field_ref, (send1, send2, send3, send4))


def split(curl_ref, matrix_ref, buf, sems):
    blocks, links, width, _ = curl_ref.shape
    groups = sems.shape[0]
    per = blocks // groups
    chunks = [pl.ds(g * per, per) for g in range(groups)]
    copies = [
        pltpu.make_async_copy(curl_ref.at[c], buf.at[c], sems.at[g]) for g, c in enumerate(chunks)
    ]
    for copy in copies:
        copy.start()
    for b in range(blocks):
        if b % per == 0:
            copies[b // per].wait()
        for k in range(links):
            high, low = halves(buf[b, k])
            matrix_ref[b, k * width : (k + 1) * width, :width] = high.T
            matrix_ref[b, k * width : (k + 1) * width, width:] = low.T


def extend(field_ref, got_refs, ext):
    blocks, rows, _ = field_ref.shape
    at = 0
    for ref in (field_ref, *got_refs):
        for t in range(ref.shape[0]):
            high, low = halves(ref[t])
            ext[at, :rows] = high
            ext[at, rows:] = low
            at += 1


def curl_row(b, links_ref, matrix_ref, ext):
    rows, width = ext.shape[1] // 2, ext.shape[2]
    x = jnp.concatenate([ext[links_ref[k, b]] for k in range(links_ref.shape[0])], axis=1)
    y = jnp.dot(x, matrix_ref[b], preferred_element_type=F32)
    return y[:rows, :width] + (y[rows:, :width] + y[:rows, width:] + y[rows:, width:])


def first(
    links_ref, tiles_ref, omega_ref, mass_ref, field_ref, matrix_ref, got1, got2, got3, got4,
    dir_ref, base_ref, send1, send2, send3, send4, ext,
):
    blocks, rows, lanes = field_ref.shape
    extend(field_ref, (got1, got2, got3, got4), ext)
    omega, real = frequency_rows(omega_ref, rows, lanes)
    sign = jnp.where(real, -omega, omega)
    for b in range(blocks):
        u = field_ref[b]
        au = curl_row(b, links_ref, matrix_ref, ext)
        au = au + sign * mass_ref[b : b + 1] * other(u)
        resid = u - au
        direction = C1 * u + C2 * resid
        dir_ref[b] = direction
        base_ref[b] = u + direction + C3 * direction + C4 * resid
    pick(tiles_ref, dir_ref, (send1, send2, send3, send4))


def second(
    scale, links_ref, omega_ref, mass_ref, dir_ref, base_ref, matrix_ref, got1, got2, got3, got4,
    cells_ref, fwd_hbm, adj_hbm, grad_ref, ext, table, fwd_ref, adj_ref, sems,
):
    blocks, rows, lanes = dir_ref.shape
    half = rows // 2
    extend(dir_ref, (got1, got2, got3, got4), ext)
    omega, real = frequency_rows(omega_ref, rows, lanes)
    sign = jnp.where(real, -omega, omega)
    for b in range(blocks):
        au = curl_row(b, links_ref, matrix_ref, ext)
        au = au + sign * mass_ref[b : b + 1] * other(dir_ref[b])
        x = base_ref[b] - C4 * au
        efield, lfield = x[:half], x[half:]
        fwd_ref[pl.ds(b, half, stride=blocks), :] = efield
        adj_ref[pl.ds(b, half, stride=blocks), :] = lfield
        prod = omega[:half] * efield * other(lfield)
        table[b : b + 1] = jnp.sum(prod, axis=0, keepdims=True)
    copies = [
        pltpu.make_async_copy(fwd_ref, fwd_hbm, sems.at[0]),
        pltpu.make_async_copy(adj_ref, adj_hbm, sems.at[1]),
    ]
    for copy in copies:
        copy.start()
    edges, cells = cells_ref.shape
    padded = -(-edges // 8) * 8
    for c in range(cells // lanes):
        index = cells_ref[:, c * lanes : (c + 1) * lanes]
        fill = jnp.full((padded - edges, lanes), -1, jnp.int32)
        index = jnp.concatenate([index, fill], axis=0)
        total = None
        for e in range(0, padded, 8):
            block, lane = index[e : e + 8] >> 7, index[e : e + 8] & 127
            found = jnp.zeros((8, lanes), F32)
            for b in range(blocks):
                row = jnp.broadcast_to(table[b : b + 1], (8, lanes))
                value = jnp.take_along_axis(row, lane, axis=1, mode="promise_in_bounds")
                found = jnp.where(block == b, value, found)
            total = found if total is None else total + found
        grad_ref[c : c + 1] = jnp.sum(total, axis=0, keepdims=True) * scale
    for copy in copies:
        copy.wait()


def local(
    fwd_source, adj_source, curl_blocks, block_links, tile_lists, edge_mass, omega, cell_edges, log_cond
):
    count, comps, blocks, lanes = fwd_source.shape
    rounds, tiles = tile_lists.shape
    links = block_links.shape[1]
    half = count * comps
    rows = 2 * half
    flat = (half * blocks, lanes)
    field_shape = pltpu.VMEM((blocks, rows, lanes), F32)
    tile_shape = pltpu.VMEM((tiles, rows, lanes), F32)
    flat_shape = pltpu.VMEM(flat, F32)
    matrix_shape = pltpu.VMEM((blocks, links * lanes, 2 * lanes), BF16)
    ext = pltpu.VMEM((blocks + rounds * tiles, 2 * rows, lanes), BF16)
    links_t = block_links.T

    field, *sends = pl.pallas_call(
        prepare,
        out_shape=[field_shape] + [tile_shape] * rounds,
        in_specs=[HB] * 3,
        out_specs=[VM] * (1 + rounds),
        scratch_shapes=[pltpu.SMEM(tile_lists.shape, jnp.int32), flat_shape, flat_shape, DMA((3,))],
        compiler_params=params(8),
        name="prepare",
    )(far(tile_lists), far(fwd_source.reshape(flat)), far(adj_source.reshape(flat)))

    def trade(sends):
        got = [None] * rounds
        for r in (2, 1, 3, 0):
            got[r] = swapped(sends[r], "dom", 2**r)
        return [near(g) for g in got]

    got = trade(sends)
    matrix = pl.pallas_call(
        split,
        out_shape=matrix_shape,
        in_specs=[HB],
        out_specs=VM,
        scratch_shapes=[pltpu.VMEM(curl_blocks.shape, F32), DMA((blocks // 4,))],
        compiler_params=params(32),
        cost_estimate=cost(8 << 20, 16 << 20),
        name="split",
    )(far(curl_blocks))
    matrix = near(matrix)
    direction, base, *sends = pl.pallas_call(
        first,
        out_shape=[field_shape] * 2 + [tile_shape] * rounds,
        in_specs=[SM] * 3 + [VM] * (3 + rounds),
        out_specs=[VM] * (2 + rounds),
        scratch_shapes=[ext],
        compiler_params=params(32),
        name="first",
    )(links_t, tile_lists, omega, edge_mass, near(field), matrix, *got)
    got = trade(sends)
    scale = 1.0 / math.sqrt(24.0 * count * lax.axis_size("freq"))
    efield, lfield, grad = pl.pallas_call(
        lambda *refs: second(scale, *refs),
        out_shape=[
            pltpu.HBM(flat, F32),
            pltpu.HBM(flat, F32),
            pltpu.VMEM((log_cond.shape[0] // lanes, lanes), F32),
        ],
        in_specs=[SM] * 2 + [VM] * (5 + rounds),
        out_specs=[HB, HB, VM],
        scratch_shapes=[ext, pltpu.VMEM((blocks, lanes), F32), flat_shape, flat_shape, DMA((2,))],
        compiler_params=params(32),
        name="second",
    )(links_t, omega, edge_mass, near(direction), near(base), matrix, *got, cell_edges)
    got = [swapped(grad, "freq", mask) for mask in (2, 6, 4)]
    grad = grad + got[0] + got[1] + got[2]
    grad = grad + swapped(grad, "freq", 1)
    grad = grad.reshape(log_cond.shape)
    model_next = log_cond - 0.5 * grad / jnp.sqrt(grad * grad + 1.0)
    shape = fwd_source.shape
    return efield.reshape(shape), lfield.reshape(shape), model_next


def solution(mesh):
    field = P("freq", None, "dom", None)
    in_specs = (
        field,
        field,
        P("dom", None, None, None),
        P("dom", None),
        P("dom", None),
        P("dom", None),
        P("freq"),
        P(None, "dom"),
        P("dom"),
    )
    out_specs = (field, field, P("dom"))
    return jax.shard_map(local, mesh=mesh, in_specs=in_specs, out_specs=out_specs, check_vma=False)
```

```python
import math

import jax
import jax.numpy as jnp
from jax import lax
from jax.experimental import pallas as pl
from jax.experimental.pallas import tpu as pltpu
from jax.sharding import PartitionSpec as P

THETA = 1.0
DELTA = 0.7
SONE = THETA / DELTA
RHO0 = 1.0 / SONE
RHO1 = 1.0 / (2.0 * SONE - RHO0)
RHO2 = 1.0 / (2.0 * SONE - RHO1)
C1, C2 = RHO1 * RHO0, 2.0 * RHO1 / DELTA
C3, C4 = RHO2 * RHO1, 2.0 * RHO2 / DELTA

ORDER = (2, 1, 3, 0)

F32, BF16 = jnp.float32, jnp.bfloat16
VM = pl.BlockSpec(memory_space=pltpu.VMEM)
SM = pl.BlockSpec(memory_space=pltpu.SMEM)
HB = pl.BlockSpec(memory_space=pltpu.HBM)
DMA = pltpu.SemaphoreType.DMA
NT = (((1,), (1,)), ((), ()))


def swapped(value, axis, mask):
    pairs = [(source, source ^ mask) for source in range(lax.axis_size(axis))]
    return lax.ppermute(value, axis, pairs)


def near(value):
    return pltpu.with_memory_space_constraint(value, pltpu.VMEM)


def far(value):
    return pltpu.with_memory_space_constraint(value, pltpu.HBM)


def params(mib):
    return pltpu.CompilerParams(vmem_limit_bytes=mib << 20)


def cost(flops, moved):
    return pl.CostEstimate(flops=flops, bytes_accessed=moved, transcendentals=0)


def halves(value):
    high = value.astype(BF16)
    return high, (value - high.astype(F32)).astype(BF16)


def other(value):
    count = value.shape[0]
    even = lax.broadcasted_iota(jnp.int32, value.shape, 0) % 2 == 0
    return jnp.where(even, pltpu.roll(value, count - 1, 0), pltpu.roll(value, 1, 0))


def frequency_rows(omega_ref, rows, lanes):
    row = lax.broadcasted_iota(jnp.int32, (rows, lanes), 0)
    count = omega_ref.shape[0]
    which = (row // 4) % count
    out = jnp.full((rows, lanes), omega_ref[0], F32)
    for f in range(1, count):
        out = jnp.where(which == f, omega_ref[f], out)
    return out, row % 2 == 0


def pick(tiles_ref, field_ref, send_refs):
    for r, send_ref in enumerate(send_refs):
        for t in range(send_ref.shape[0]):
            send_ref[t] = field_ref[tiles_ref[r, t]]


def prepare(
    tiles_hbm, fwd_hbm, adj_hbm, field_ref, send1, send2, send3, send4, tiles_ref, fwd_ref, adj_ref, sems
):
    blocks, rows, _ = field_ref.shape
    half = rows // 2
    pairs = ((tiles_hbm, tiles_ref), (fwd_hbm, fwd_ref), (adj_hbm, adj_ref))
    copies = [pltpu.make_async_copy(a, b, sems.at[i]) for i, (a, b) in enumerate(pairs)]
    for copy in copies:
        copy.start()
    for copy in copies:
        copy.wait()
    for b in range(blocks):
        field_ref[b, :half] = fwd_ref[pl.ds(b, half, stride=blocks), :]
        field_ref[b, half:] = adj_ref[pl.ds(b, half, stride=blocks), :]
    pick(tiles_ref, field_ref, (send1, send2, send3, send4))


def split(curl_ref, matrix_ref):
    blocks, links, width, _ = curl_ref.shape
    for b in range(blocks):
        for k in range(links):
            high, low = halves(curl_ref[b, k])
            matrix_ref[b, k * width : (k + 1) * width, :width] = high.T
            matrix_ref[b, k * width : (k + 1) * width, width:] = low.T


def extend(rows, refs, ext, at=0):
    for ref in refs:
        for t in range(ref.shape[0]):
            high, low = halves(ref[t])
            ext[at, :rows] = high
            ext[at, rows:] = low
            at += 1


def by_round(got_refs):
    got = dict(zip(ORDER, got_refs))
    return [got[r] for r in range(len(ORDER))]


def product(x, matrix):
    rows, width = x.shape[0] // 2, matrix.shape[1] // 2
    y = jnp.dot(x, matrix, preferred_element_type=F32)
    return y[:rows, :width] + (y[rows:, :width] + y[:rows, width:] + y[rows:, width:])


def curl_row(b, links_ref, matrix_ref, ext, start=0):
    links, width = links_ref.shape[0], ext.shape[2]
    x = jnp.concatenate([ext[links_ref[k, b]] for k in range(start, links)], axis=1)
    return product(x, matrix_ref[b, start * width :])


def first(
    links_ref, tiles_ref, omega_ref, mass_ref, field_ref, matrix_ref, got1, got2, got3, got4,
    dir_ref, base_ref, send1, send2, send3, send4, ext,
):
    blocks, rows, lanes = field_ref.shape
    extend(rows, [field_ref] + by_round((got1, got2, got3, got4)), ext)
    omega, real = frequency_rows(omega_ref, rows, lanes)
    sign = jnp.where(real, -omega, omega)
    for b in range(blocks):
        u = field_ref[b]
        au = curl_row(b, links_ref, matrix_ref, ext)
        au = au + sign * mass_ref[b : b + 1] * other(u)
        resid = u - au
        direction = C1 * u + C2 * resid
        dir_ref[b] = direction
        base_ref[b] = u + direction + C3 * direction + C4 * resid
    pick(tiles_ref, dir_ref, (send1, send2, send3, send4))


def middle(omega_ref, mass_ref, dir_ref, base_ref, matrix_ref, rest_ref, ext_ref):
    blocks, rows, lanes = dir_ref.shape
    omega, real = frequency_rows(omega_ref, rows, lanes)
    sign = jnp.where(real, -omega, omega)
    for b in range(blocks):
        u = dir_ref[b]
        high, low = halves(u)
        x = jnp.concatenate([high, low], axis=0)
        ext_ref[b] = x
        au = product(x, matrix_ref[b, :lanes]) + sign * mass_ref[b : b + 1] * other(u)
        rest_ref[b] = base_ref[b] - C4 * au


def second(
    scale, links_ref, omega_ref, own_ref, rest_ref, matrix_ref, got1, got2, got3, got4,
    cells_ref, fwd_ref, adj_ref, grad_ref, ext, table,
):
    blocks, rows, lanes = rest_ref.shape
    half = rows // 2
    ext[:blocks] = own_ref[...]
    extend(rows, by_round((got1, got2, got3, got4)), ext, blocks)
    omega, _ = frequency_rows(omega_ref, rows, lanes)
    for b in range(blocks):
        x = rest_ref[b] - C4 * curl_row(b, links_ref, matrix_ref, ext, 1)
        efield, lfield = x[:half], x[half:]
        fwd_ref[pl.ds(b, half, stride=blocks), :] = efield
        adj_ref[pl.ds(b, half, stride=blocks), :] = lfield
        prod = omega[:half] * efield * other(lfield)
        table[b : b + 1] = jnp.sum(prod, axis=0, keepdims=True)
    edges, cells = cells_ref.shape
    padded = -(-edges // 8) * 8
    for c in range(cells // lanes):
        index = cells_ref[:, c * lanes : (c + 1) * lanes]
        fill = jnp.full((padded - edges, lanes), -1, jnp.int32)
        index = jnp.concatenate([index, fill], axis=0)
        total = None
        for e in range(0, padded, 8):
            block, lane = index[e : e + 8] >> 7, index[e : e + 8] & 127
            found = jnp.zeros((8, lanes), F32)
            for b in range(blocks):
                row = jnp.broadcast_to(table[b : b + 1], (8, lanes))
                value = jnp.take_along_axis(row, lane, axis=1, mode="promise_in_bounds")
                found = jnp.where(block == b, value, found)
            total = found if total is None else total + found
        grad_ref[c : c + 1] = jnp.sum(total, axis=0, keepdims=True) * scale


def store(fwd_ref, adj_ref, fwd_hbm, adj_hbm, sems):
    pairs = ((fwd_ref, fwd_hbm), (adj_ref, adj_hbm))
    copies = [pltpu.make_async_copy(a, b, sems.at[i]) for i, (a, b) in enumerate(pairs)]
    for copy in copies:
        copy.start()
    for copy in copies:
        copy.wait()


def local(
    fwd_source, adj_source, curl_blocks, block_links, tile_lists, edge_mass, omega, cell_edges, log_cond
):
    count, comps, blocks, lanes = fwd_source.shape
    rounds, tiles = tile_lists.shape
    links = block_links.shape[1]
    half = count * comps
    rows = 2 * half
    flat = (half * blocks, lanes)
    field_shape = pltpu.VMEM((blocks, rows, lanes), F32)
    tile_shape = pltpu.VMEM((tiles, rows, lanes), F32)
    flat_shape = pltpu.VMEM(flat, F32)
    matrix_shape = pltpu.VMEM((blocks, links * lanes, 2 * lanes), BF16)
    ext = pltpu.VMEM((blocks + rounds * tiles, 2 * rows, lanes), BF16)
    links_t = block_links.T

    field, *sends = pl.pallas_call(
        prepare,
        out_shape=[field_shape] + [tile_shape] * rounds,
        in_specs=[HB] * 3,
        out_specs=[VM] * (1 + rounds),
        scratch_shapes=[pltpu.SMEM(tile_lists.shape, jnp.int32), flat_shape, flat_shape, DMA((3,))],
        compiler_params=params(8),
        cost_estimate=cost(3 << 30, 1 << 20),
        name="prepare",
    )(far(tile_lists), far(fwd_source.reshape(flat)), far(adj_source.reshape(flat)))

    def trade(sends):
        return [near(swapped(sends[r], "dom", 2**r)) for r in ORDER]

    got = trade(sends)
    matrix = pl.pallas_call(
        split,
        out_shape=matrix_shape,
        in_specs=[VM],
        out_specs=VM,
        compiler_params=params(32),
        cost_estimate=cost(8 << 20, 16 << 20),
        name="split",
    )(curl_blocks)
    matrix = near(matrix)
    direction, base, *sends = pl.pallas_call(
        first,
        out_shape=[field_shape] * 2 + [tile_shape] * rounds,
        in_specs=[SM] * 3 + [VM] * (3 + rounds),
        out_specs=[VM] * (2 + rounds),
        scratch_shapes=[ext],
        compiler_params=params(32),
        name="first",
    )(links_t, tile_lists, omega, edge_mass, near(field), matrix, *got)
    got = trade(sends)
    rest, own = pl.pallas_call(
        middle,
        out_shape=[field_shape, pltpu.VMEM((blocks, 2 * rows, lanes), BF16)],
        in_specs=[SM] + [VM] * 4,
        out_specs=[VM] * 2,
        compiler_params=params(32),
        cost_estimate=cost(1 << 20, 4 << 20),
        name="middle",
    )(omega, edge_mass, near(direction), near(base), matrix)
    scale = 1.0 / math.sqrt(24.0 * count * lax.axis_size("freq"))
    efield, lfield, grad = pl.pallas_call(
        lambda *refs: second(scale, *refs),
        out_shape=[
            flat_shape,
            flat_shape,
            pltpu.VMEM((log_cond.shape[0] // lanes, lanes), F32),
        ],
        in_specs=[SM] * 2 + [VM] * (4 + rounds),
        out_specs=[VM] * 3,
        scratch_shapes=[ext, pltpu.VMEM((blocks, lanes), F32)],
        compiler_params=params(32),
        name="second",
    )(links_t, omega, near(own), near(rest), matrix, *got, cell_edges)
    efield, lfield = pl.pallas_call(
        store,
        out_shape=[pltpu.HBM(flat, F32)] * 2,
        in_specs=[VM] * 2,
        out_specs=[HB] * 2,
        scratch_shapes=[DMA((2,))],
        compiler_params=params(8),
        cost_estimate=cost(1 << 10, 1 << 20),
        name="store",
    )(near(efield), near(lfield))
    got = [swapped(grad, "freq", mask) for mask in (2, 6, 4)]
    grad = grad + got[0] + got[1] + got[2]
    grad = grad + swapped(grad, "freq", 1)
    grad = grad.reshape(log_cond.shape)
    model_next = log_cond - 0.5 * grad / jnp.sqrt(grad * grad + 1.0)
    shape = fwd_source.shape
    return efield.reshape(shape), lfield.reshape(shape), model_next


def solution(mesh):
    field = P("freq", None, "dom", None)
    in_specs = (
        field,
        field,
        P("dom", None, None, None),
        P("dom", None),
        P("dom", None),
        P("dom", None),
        P("freq"),
        P(None, "dom"),
        P("dom"),
    )
    out_specs = (field, field, P("dom"))
    return jax.shard_map(local, mesh=mesh, in_specs=in_specs, out_specs=out_specs, check_vma=False)
```

```python
import math

import jax
import jax.numpy as jnp
from jax import lax
from jax.experimental import pallas as pl
from jax.experimental.pallas import tpu as pltpu
from jax.sharding import PartitionSpec as P

THETA = 1.0
DELTA = 0.7
SONE = THETA / DELTA
RHO0 = 1.0 / SONE
RHO1 = 1.0 / (2.0 * SONE - RHO0)
RHO2 = 1.0 / (2.0 * SONE - RHO1)
C1, C2 = RHO1 * RHO0, 2.0 * RHO1 / DELTA
C3, C4 = RHO2 * RHO1, 2.0 * RHO2 / DELTA

ORDER = (2, 1, 3, 0)

F32, BF16 = jnp.float32, jnp.bfloat16
VM = pl.BlockSpec(memory_space=pltpu.VMEM)
SM = pl.BlockSpec(memory_space=pltpu.SMEM)
HB = pl.BlockSpec(memory_space=pltpu.HBM)
DMA = pltpu.SemaphoreType.DMA
NT = (((1,), (1,)), ((), ()))


def swapped(value, axis, mask):
    pairs = [(source, source ^ mask) for source in range(lax.axis_size(axis))]
    return lax.ppermute(value, axis, pairs)


def near(value):
    return pltpu.with_memory_space_constraint(value, pltpu.VMEM)


def far(value):
    return pltpu.with_memory_space_constraint(value, pltpu.HBM)


def params(mib):
    return pltpu.CompilerParams(vmem_limit_bytes=mib << 20)


def cost(flops, moved):
    return pl.CostEstimate(flops=flops, bytes_accessed=moved, transcendentals=0)


def halves(value):
    high = value.astype(BF16)
    return high, (value - high.astype(F32)).astype(BF16)


def other(value):
    count = value.shape[0]
    even = lax.broadcasted_iota(jnp.int32, value.shape, 0) % 2 == 0
    return jnp.where(even, pltpu.roll(value, count - 1, 0), pltpu.roll(value, 1, 0))


def frequency_rows(omega_ref, rows, lanes):
    row = lax.broadcasted_iota(jnp.int32, (rows, lanes), 0)
    count = omega_ref.shape[0]
    which = (row // 4) % count
    out = jnp.full((rows, lanes), omega_ref[0], F32)
    for f in range(1, count):
        out = jnp.where(which == f, omega_ref[f], out)
    return out, row % 2 == 0


def pick(tiles_ref, field_ref, send_refs):
    for r, send_ref in enumerate(send_refs):
        for t in range(send_ref.shape[0]):
            send_ref[t] = field_ref[tiles_ref[r, t]]


def prepare(
    tiles_hbm, fwd_hbm, adj_hbm, field_ref, send1, send2, send3, send4, tiles_ref, fwd_ref, adj_ref, sems
):
    blocks, rows, _ = field_ref.shape
    half = rows // 2
    pairs = ((tiles_hbm, tiles_ref), (fwd_hbm, fwd_ref), (adj_hbm, adj_ref))
    copies = [pltpu.make_async_copy(a, b, sems.at[i]) for i, (a, b) in enumerate(pairs)]
    for copy in copies:
        copy.start()
    for copy in copies:
        copy.wait()
    for b in range(blocks):
        field_ref[b, :half] = fwd_ref[pl.ds(b, half, stride=blocks), :]
        field_ref[b, half:] = adj_ref[pl.ds(b, half, stride=blocks), :]
    pick(tiles_ref, field_ref, (send1, send2, send3, send4))


def split(omega_ref, mass_ref, field_ref, curl_ref, matrix_ref, rest_ref, ext_ref):
    blocks, links, width, _ = curl_ref.shape
    rows, lanes = field_ref.shape[1:]
    sign = signs(omega_ref, rows, lanes)
    for b in range(blocks):
        for k in range(links):
            high, low = halves(curl_ref[b, k])
            both = jnp.concatenate([high.T, low.T], axis=1)
            matrix_ref[b, k * width : (k + 1) * width] = both
            if k == 0:
                own_row(b, 1.0, sign, both, mass_ref, field_ref, field_ref, rest_ref, ext_ref)


def extend(rows, refs, ext, at=0):
    for ref in refs:
        for t in range(ref.shape[0]):
            high, low = halves(ref[t])
            ext[at, :rows] = high
            ext[at, rows:] = low
            at += 1


def by_round(got_refs):
    got = dict(zip(ORDER, got_refs))
    return [got[r] for r in range(len(ORDER))]


def product(x, matrix):
    rows, width = x.shape[0] // 2, matrix.shape[1] // 2
    y = jnp.dot(x, matrix, preferred_element_type=F32)
    return y[:rows, :width] + (y[rows:, :width] + y[:rows, width:] + y[rows:, width:])


def curl_row(b, links_ref, matrix_ref, ext, start=0):
    links, width = links_ref.shape[0], ext.shape[2]
    x = jnp.concatenate([ext[links_ref[k, b]] for k in range(start, links)], axis=1)
    return product(x, matrix_ref[b, start * width :])


def signs(omega_ref, rows, lanes):
    omega, real = frequency_rows(omega_ref, rows, lanes)
    return jnp.where(real, -omega, omega)


def own_row(b, scale, sign, matrix, mass_ref, field_ref, start_ref, rest_ref, ext_ref):
    u = field_ref[b]
    x = jnp.concatenate(halves(u), axis=0)
    ext_ref[b] = x
    au = product(x, matrix) + sign * mass_ref[b : b + 1] * other(u)
    rest_ref[b] = start_ref[b] - scale * au


def middle(scale, omega_ref, mass_ref, field_ref, start_ref, matrix_ref, rest_ref, ext_ref):
    blocks, rows, lanes = field_ref.shape
    sign = signs(omega_ref, rows, lanes)
    for b in range(blocks):
        own_row(
            b, scale, sign, matrix_ref[b, :lanes], mass_ref, field_ref, start_ref, rest_ref, ext_ref
        )


def first(
    links_ref, tiles_ref, field_ref, own_ref, rest_ref, matrix_ref, got1, got2, got3, got4,
    dir_ref, base_ref, send1, send2, send3, send4, ext,
):
    blocks, rows, _ = field_ref.shape
    ext[:blocks] = own_ref[...]
    extend(rows, by_round((got1, got2, got3, got4)), ext, blocks)
    for b in range(blocks):
        resid = rest_ref[b] - curl_row(b, links_ref, matrix_ref, ext, 1)
        direction = C1 * field_ref[b] + C2 * resid
        dir_ref[b] = direction
        base_ref[b] = field_ref[b] + direction + C3 * direction + C4 * resid
    pick(tiles_ref, dir_ref, (send1, send2, send3, send4))


def second(
    scale, links_ref, omega_ref, own_ref, rest_ref, matrix_ref, got1, got2, got3, got4,
    cells_ref, fwd_ref, adj_ref, grad_ref, ext, table,
):
    blocks, rows, lanes = rest_ref.shape
    half = rows // 2
    ext[:blocks] = own_ref[...]
    extend(rows, by_round((got1, got2, got3, got4)), ext, blocks)
    omega, _ = frequency_rows(omega_ref, rows, lanes)
    for b in range(blocks):
        x = rest_ref[b] - C4 * curl_row(b, links_ref, matrix_ref, ext, 1)
        efield, lfield = x[:half], x[half:]
        fwd_ref[pl.ds(b, half, stride=blocks), :] = efield
        adj_ref[pl.ds(b, half, stride=blocks), :] = lfield
        prod = omega[:half] * efield * other(lfield)
        table[b : b + 1] = jnp.sum(prod, axis=0, keepdims=True)
    edges, cells = cells_ref.shape

    def find(index):
        block, lane = index >> 7, index & 127
        found = jnp.zeros(index.shape, F32)
        for b in range(blocks):
            row = jnp.broadcast_to(table[b : b + 1], index.shape)
            value = jnp.take_along_axis(row, lane, axis=1, mode="promise_in_bounds")
            found = jnp.where(block == b, value, found)
        return found

    def total(found):
        return jnp.sum(found, axis=0, keepdims=True)

    for c in range(0, cells // lanes, 2):
        left = cells_ref[:, c * lanes : (c + 1) * lanes]
        right = cells_ref[:, (c + 1) * lanes : (c + 2) * lanes]
        last = find(jnp.concatenate([left[8:], right[8:]], axis=0))
        grad_ref[c : c + 1] = (total(find(left[:8])) + total(last[: edges - 8])) * scale
        grad_ref[c + 1 : c + 2] = (total(find(right[:8])) + total(last[edges - 8 :])) * scale


def store(fwd_ref, adj_ref, fwd_hbm, adj_hbm, sems):
    pairs = ((fwd_ref, fwd_hbm), (adj_ref, adj_hbm))
    copies = [pltpu.make_async_copy(a, b, sems.at[i]) for i, (a, b) in enumerate(pairs)]
    for copy in copies:
        copy.start()
    for copy in copies:
        copy.wait()


def local(
    fwd_source, adj_source, curl_blocks, block_links, tile_lists, edge_mass, omega, cell_edges, log_cond
):
    count, comps, blocks, lanes = fwd_source.shape
    rounds, tiles = tile_lists.shape
    links = block_links.shape[1]
    half = count * comps
    rows = 2 * half
    flat = (half * blocks, lanes)
    field_shape = pltpu.VMEM((blocks, rows, lanes), F32)
    tile_shape = pltpu.VMEM((tiles, rows, lanes), F32)
    flat_shape = pltpu.VMEM(flat, F32)
    matrix_shape = pltpu.VMEM((blocks, links * lanes, 2 * lanes), BF16)
    ext = pltpu.VMEM((blocks + rounds * tiles, 2 * rows, lanes), BF16)
    links_t = block_links.T

    field, *sends = pl.pallas_call(
        prepare,
        out_shape=[field_shape] + [tile_shape] * rounds,
        in_specs=[HB] * 3,
        out_specs=[VM] * (1 + rounds),
        scratch_shapes=[pltpu.SMEM(tile_lists.shape, jnp.int32), flat_shape, flat_shape, DMA((3,))],
        compiler_params=params(8),
        cost_estimate=cost(3 << 30, 1 << 20),
        name="prepare",
    )(far(tile_lists), far(fwd_source.reshape(flat)), far(adj_source.reshape(flat)))

    def trade(sends):
        return [near(swapped(sends[r], "dom", 2**r)) for r in ORDER]

    got = trade(sends)
    own_shape = pltpu.VMEM((blocks, 2 * rows, lanes), BF16)
    field = near(field)
    matrix, rest, own = [
        near(out)
        for out in pl.pallas_call(
            split,
            out_shape=[matrix_shape, field_shape, own_shape],
            in_specs=[SM] + [VM] * 3,
            out_specs=[VM] * 3,
            compiler_params=params(32),
            cost_estimate=cost(8 << 20, 16 << 20),
            name="split",
        )(omega, edge_mass, field, curl_blocks)
    ]
    direction, base, *sends = pl.pallas_call(
        first,
        out_shape=[field_shape] * 2 + [tile_shape] * rounds,
        in_specs=[SM] * 2 + [VM] * (4 + rounds),
        out_specs=[VM] * (2 + rounds),
        scratch_shapes=[ext],
        compiler_params=params(32),
        name="first",
    )(links_t, tile_lists, field, own, rest, matrix, *got)
    got = trade(sends)
    rest, own = [
        near(out)
        for out in pl.pallas_call(
            lambda *refs: middle(C4, *refs),
            out_shape=[field_shape, own_shape],
            in_specs=[SM] + [VM] * 4,
            out_specs=[VM] * 2,
            compiler_params=params(32),
            cost_estimate=cost(1 << 20, 4 << 20),
            name="middle",
        )(omega, edge_mass, near(direction), near(base), matrix)
    ]
    scale = 1.0 / math.sqrt(24.0 * count * lax.axis_size("freq"))
    efield, lfield, grad = pl.pallas_call(
        lambda *refs: second(scale, *refs),
        out_shape=[
            flat_shape,
            flat_shape,
            pltpu.VMEM((log_cond.shape[0] // lanes, lanes), F32),
        ],
        in_specs=[SM] * 2 + [VM] * (4 + rounds),
        out_specs=[VM] * 3,
        scratch_shapes=[ext, pltpu.VMEM((blocks, lanes), F32)],
        compiler_params=params(32),
        name="second",
    )(links_t, omega, own, rest, matrix, *got, cell_edges)
    efield, lfield = pl.pallas_call(
        store,
        out_shape=[pltpu.HBM(flat, F32)] * 2,
        in_specs=[VM] * 2,
        out_specs=[HB] * 2,
        scratch_shapes=[DMA((2,))],
        compiler_params=params(8),
        cost_estimate=cost(1 << 10, 1 << 20),
        name="store",
    )(near(efield), near(lfield))
    got = [swapped(grad, "freq", mask) for mask in (2, 6, 4)]
    grad = grad + got[0] + got[1] + got[2]
    grad = grad + swapped(grad, "freq", 1)
    grad = grad.reshape(log_cond.shape)
    model_next = log_cond - 0.5 * grad / jnp.sqrt(grad * grad + 1.0)
    shape = fwd_source.shape
    return efield.reshape(shape), lfield.reshape(shape), model_next


def solution(mesh):
    field = P("freq", None, "dom", None)
    in_specs = (
        field,
        field,
        P("dom", None, None, None),
        P("dom", None),
        P("dom", None),
        P("dom", None),
        P("freq"),
        P(None, "dom"),
        P("dom"),
    )
    out_specs = (field, field, P("dom"))
    return jax.shard_map(local, mesh=mesh, in_specs=in_specs, out_specs=out_specs, check_vma=False)
```

```python
import math

import jax
import jax.numpy as jnp
from jax import lax
from jax.experimental import pallas as pl
from jax.experimental.pallas import tpu as pltpu
from jax.sharding import PartitionSpec as P

THETA = 1.0
DELTA = 0.7
SONE = THETA / DELTA
RHO0 = 1.0 / SONE
RHO1 = 1.0 / (2.0 * SONE - RHO0)
RHO2 = 1.0 / (2.0 * SONE - RHO1)
C1, C2 = RHO1 * RHO0, 2.0 * RHO1 / DELTA
C3, C4 = RHO2 * RHO1, 2.0 * RHO2 / DELTA

ORDER = (2, 1, 3, 0)

F32, BF16 = jnp.float32, jnp.bfloat16
VM = pl.BlockSpec(memory_space=pltpu.VMEM)
SM = pl.BlockSpec(memory_space=pltpu.SMEM)
HB = pl.BlockSpec(memory_space=pltpu.HBM)
DMA = pltpu.SemaphoreType.DMA
NT = (((1,), (1,)), ((), ()))


def swapped(value, axis, mask):
    pairs = [(source, source ^ mask) for source in range(lax.axis_size(axis))]
    return lax.ppermute(value, axis, pairs)


def near(value):
    return pltpu.with_memory_space_constraint(value, pltpu.VMEM)


def far(value):
    return pltpu.with_memory_space_constraint(value, pltpu.HBM)


def params(mib):
    return pltpu.CompilerParams(vmem_limit_bytes=mib << 20)


def cost(flops, moved):
    return pl.CostEstimate(flops=flops, bytes_accessed=moved, transcendentals=0)


def halves(value):
    high = value.astype(BF16)
    return high, (value - high.astype(F32)).astype(BF16)


def other(value):
    count = value.shape[0]
    even = lax.broadcasted_iota(jnp.int32, value.shape, 0) % 2 == 0
    return jnp.where(even, pltpu.roll(value, count - 1, 0), pltpu.roll(value, 1, 0))


def frequency_rows(omega_ref, rows, lanes):
    row = lax.broadcasted_iota(jnp.int32, (rows, lanes), 0)
    count = omega_ref.shape[0]
    which = (row // 4) % count
    out = jnp.full((rows, lanes), omega_ref[0], F32)
    for f in range(1, count):
        out = jnp.where(which == f, omega_ref[f], out)
    return out, row % 2 == 0


def pick(tiles_ref, field_ref, send_refs):
    for r, send_ref in enumerate(send_refs):
        for t in range(send_ref.shape[0]):
            send_ref[t] = field_ref[tiles_ref[r, t]]


def prepare(
    tiles_hbm, fwd_hbm, adj_hbm, field_ref, send1, send2, send3, send4, tiles_ref, fwd_ref, adj_ref, sems
):
    blocks, rows, _ = field_ref.shape
    half = rows // 2
    pairs = ((tiles_hbm, tiles_ref), (fwd_hbm, fwd_ref), (adj_hbm, adj_ref))
    copies = [pltpu.make_async_copy(a, b, sems.at[i]) for i, (a, b) in enumerate(pairs)]
    for copy in copies:
        copy.start()
    for copy in copies:
        copy.wait()
    for b in range(blocks):
        field_ref[b, :half] = fwd_ref[pl.ds(b, half, stride=blocks), :]
        field_ref[b, half:] = adj_ref[pl.ds(b, half, stride=blocks), :]
    pick(tiles_ref, field_ref, (send1, send2, send3, send4))


def split(omega_ref, mass_ref, field_ref, curl_ref, matrix_ref, rest_ref, ext_ref):
    blocks, links, width, _ = curl_ref.shape
    rows, lanes = field_ref.shape[1:]
    sign = signs(omega_ref, rows, lanes)
    for b in range(blocks):
        for k in range(links):
            high, low = halves(curl_ref[b, k])
            both = jnp.concatenate([high.T, low.T], axis=1)
            matrix_ref[b, k * width : (k + 1) * width] = both
            if k == 0:
                own_row(b, 1.0, sign, both, mass_ref, field_ref, field_ref, rest_ref, ext_ref)


def extend(rows, refs, ext, at=0):
    for ref in refs:
        for t in range(ref.shape[0]):
            high, low = halves(ref[t])
            ext[at, :rows] = high
            ext[at, rows:] = low
            at += 1


def by_round(got_refs):
    got = dict(zip(ORDER, got_refs))
    return [got[r] for r in range(len(ORDER))]


def product(x, matrix):
    rows, width = x.shape[0] // 2, matrix.shape[1] // 2
    y = jnp.dot(x, matrix, preferred_element_type=F32)
    return y[:rows, :width] + (y[rows:, :width] + y[:rows, width:] + y[rows:, width:])


def curl_row(b, links_ref, matrix_ref, ext, start=0):
    links, width = links_ref.shape[0], ext.shape[2]
    x = jnp.concatenate([ext[links_ref[k, b]] for k in range(start, links)], axis=1)
    return product(x, matrix_ref[b, start * width :])


def signs(omega_ref, rows, lanes):
    omega, real = frequency_rows(omega_ref, rows, lanes)
    return jnp.where(real, -omega, omega)


def own_row(b, scale, sign, matrix, mass_ref, field_ref, start_ref, rest_ref, ext_ref):
    u = field_ref[b]
    x = jnp.concatenate(halves(u), axis=0)
    ext_ref[b] = x
    au = product(x, matrix) + sign * mass_ref[b : b + 1] * other(u)
    rest_ref[b] = start_ref[b] - scale * au


def middle(scale, omega_ref, mass_ref, field_ref, start_ref, matrix_ref, rest_ref, ext_ref):
    blocks, rows, lanes = field_ref.shape
    sign = signs(omega_ref, rows, lanes)
    for b in range(blocks):
        own_row(
            b, scale, sign, matrix_ref[b, :lanes], mass_ref, field_ref, start_ref, rest_ref, ext_ref
        )


def first(
    links_ref, tiles_ref, field_ref, own_ref, rest_ref, matrix_ref, got1, got2, got3, got4,
    dir_ref, base_ref, send1, send2, send3, send4, ext,
):
    blocks, rows, _ = field_ref.shape
    ext[:blocks] = own_ref[...]
    extend(rows, by_round((got1, got2, got3, got4)), ext, blocks)
    for b in range(blocks):
        resid = rest_ref[b] - curl_row(b, links_ref, matrix_ref, ext, 1)
        direction = C1 * field_ref[b] + C2 * resid
        dir_ref[b] = direction
        base_ref[b] = field_ref[b] + direction + C3 * direction + C4 * resid
    pick(tiles_ref, dir_ref, (send1, send2, send3, send4))


def second(
    scale, links_ref, omega_ref, own_ref, rest_ref, matrix_ref, got1, got2, got3, got4,
    cells_ref, field_ref, grad_ref, ext, table,
):
    blocks, rows, lanes = rest_ref.shape
    half = rows // 2
    ext[:blocks] = own_ref[...]
    extend(rows, by_round((got1, got2, got3, got4)), ext, blocks)
    omega, _ = frequency_rows(omega_ref, rows, lanes)
    for b in range(blocks):
        x = rest_ref[b] - C4 * curl_row(b, links_ref, matrix_ref, ext, 1)
        field_ref[b] = x
        prod = omega[:half] * x[:half] * other(x[half:])
        table[b : b + 1] = jnp.sum(prod, axis=0, keepdims=True)
    edges, cells = cells_ref.shape

    def find(index):
        block, lane = index >> 7, index & 127
        found = jnp.zeros(index.shape, F32)
        for b in range(blocks):
            row = jnp.broadcast_to(table[b : b + 1], index.shape)
            value = jnp.take_along_axis(row, lane, axis=1, mode="promise_in_bounds")
            found = jnp.where(block == b, value, found)
        return found

    def total(found):
        return jnp.sum(found, axis=0, keepdims=True)

    for c in range(0, cells // lanes, 2):
        left = cells_ref[:, c * lanes : (c + 1) * lanes]
        right = cells_ref[:, (c + 1) * lanes : (c + 2) * lanes]
        last = find(jnp.concatenate([left[8:], right[8:]], axis=0))
        grad_ref[c : c + 1] = (total(find(left[:8])) + total(last[: edges - 8])) * scale
        grad_ref[c + 1 : c + 2] = (total(find(right[:8])) + total(last[edges - 8 :])) * scale


def store(field_ref, fwd_hbm, adj_hbm, fwd_ref, adj_ref, sems):
    blocks, rows, _ = field_ref.shape
    half = rows // 2
    pairs = ((fwd_ref, fwd_hbm), (adj_ref, adj_hbm))
    copies = [pltpu.make_async_copy(a, b, sems.at[i]) for i, (a, b) in enumerate(pairs)]
    for s in range(2):
        for b in range(blocks):
            pairs[s][0][pl.ds(b, half, stride=blocks), :] = field_ref[b, s * half : (s + 1) * half]
        copies[s].start()
    for copy in copies:
        copy.wait()


def local(
    fwd_source, adj_source, curl_blocks, block_links, tile_lists, edge_mass, omega, cell_edges, log_cond
):
    count, comps, blocks, lanes = fwd_source.shape
    rounds, tiles = tile_lists.shape
    links = block_links.shape[1]
    half = count * comps
    rows = 2 * half
    flat = (half * blocks, lanes)
    field_shape = pltpu.VMEM((blocks, rows, lanes), F32)
    tile_shape = pltpu.VMEM((tiles, rows, lanes), F32)
    flat_shape = pltpu.VMEM(flat, F32)
    matrix_shape = pltpu.VMEM((blocks, links * lanes, 2 * lanes), BF16)
    ext = pltpu.VMEM((blocks + rounds * tiles, 2 * rows, lanes), BF16)
    links_t = block_links.T

    field, *sends = pl.pallas_call(
        prepare,
        out_shape=[field_shape] + [tile_shape] * rounds,
        in_specs=[HB] * 3,
        out_specs=[VM] * (1 + rounds),
        scratch_shapes=[pltpu.SMEM(tile_lists.shape, jnp.int32), flat_shape, flat_shape, DMA((3,))],
        compiler_params=params(8),
        cost_estimate=cost(3 << 30, 1 << 20),
        name="prepare",
    )(far(tile_lists), far(fwd_source.reshape(flat)), far(adj_source.reshape(flat)))

    def trade(sends):
        return [near(swapped(sends[r], "dom", 2**r)) for r in ORDER]

    got = trade(sends)
    own_shape = pltpu.VMEM((blocks, 2 * rows, lanes), BF16)
    field = near(field)
    matrix, rest, own = [
        near(out)
        for out in pl.pallas_call(
            split,
            out_shape=[matrix_shape, field_shape, own_shape],
            in_specs=[SM] + [VM] * 3,
            out_specs=[VM] * 3,
            compiler_params=params(32),
            cost_estimate=cost(8 << 20, 16 << 20),
            name="split",
        )(omega, edge_mass, field, curl_blocks)
    ]
    direction, base, *sends = pl.pallas_call(
        first,
        out_shape=[field_shape] * 2 + [tile_shape] * rounds,
        in_specs=[SM] * 2 + [VM] * (4 + rounds),
        out_specs=[VM] * (2 + rounds),
        scratch_shapes=[ext],
        compiler_params=params(32),
        name="first",
    )(links_t, tile_lists, field, own, rest, matrix, *got)
    got = trade(sends)
    rest, own = [
        near(out)
        for out in pl.pallas_call(
            lambda *refs: middle(C4, *refs),
            out_shape=[field_shape, own_shape],
            in_specs=[SM] + [VM] * 4,
            out_specs=[VM] * 2,
            compiler_params=params(32),
            cost_estimate=cost(1 << 20, 4 << 20),
            name="middle",
        )(omega, edge_mass, near(direction), near(base), matrix)
    ]
    scale = 1.0 / math.sqrt(24.0 * count * lax.axis_size("freq"))
    fields, grad = pl.pallas_call(
        lambda *refs: second(scale, *refs),
        out_shape=[
            field_shape,
            pltpu.VMEM((log_cond.shape[0] // lanes, lanes), F32),
        ],
        in_specs=[SM] * 2 + [VM] * (4 + rounds),
        out_specs=[VM] * 2,
        scratch_shapes=[ext, pltpu.VMEM((blocks, lanes), F32)],
        compiler_params=params(32),
        name="second",
    )(links_t, omega, own, rest, matrix, *got, cell_edges)
    efield, lfield = pl.pallas_call(
        store,
        out_shape=[pltpu.HBM(flat, F32)] * 2,
        in_specs=[VM],
        out_specs=[HB] * 2,
        scratch_shapes=[flat_shape, flat_shape, DMA((2,))],
        compiler_params=params(8),
        cost_estimate=cost(1 << 10, 1 << 20),
        name="store",
    )(near(fields))
    got = [swapped(grad, "freq", mask) for mask in (2, 6, 4)]
    grad = grad + got[0] + got[1] + got[2]
    grad = grad + swapped(grad, "freq", 1)
    grad = grad.reshape(log_cond.shape)
    model_next = log_cond - 0.5 * grad / jnp.sqrt(grad * grad + 1.0)
    shape = fwd_source.shape
    return efield.reshape(shape), lfield.reshape(shape), model_next


def solution(mesh):
    field = P("freq", None, "dom", None)
    in_specs = (
        field,
        field,
        P("dom", None, None, None),
        P("dom", None),
        P("dom", None),
        P("dom", None),
        P("freq"),
        P(None, "dom"),
        P("dom"),
    )
    out_specs = (field, field, P("dom"))
    return jax.shard_map(local, mesh=mesh, in_specs=in_specs, out_specs=out_specs, check_vma=False)
```
